32 devices in a mesh: gx: 4 (over x, core), gy: 8 (over z, y).
Axes of the slice: x: 2, y: 2, z: 4, core: 2. Of those that a mesh axis runs over, the one named last changes fastest.
Arguments:
- fine_nodes: bfloat16 [4, 8, 512, 128], P('gx', 'gy'), may hold values from -6 to 6
- fine_edges: int32 [4, 8, 2, 1536], P('gx', 'gy'), may hold values from 0 to 1023, as said below
- fine_live: int32 [4, 8], P('gx', 'gy'), may hold values from 512 to 1536, as said below
- fine_halo: int32 [4, 8, 4, 1], P('gx', 'gy'), may hold values from 0 to 3, as said below
- pool_map: int32 [4, 8, 512], P('gx', 'gy'), may hold values from 0 to 255, as said below
- coarse_edges: int32 [4, 8, 2, 2048], P('gx', 'gy'), may hold values from 0 to 767, as said below
- coarse_halo: int32 [4, 8, 4, 1], P('gx', 'gy'), may hold values from 0 to 1, as said below
- fine_weights: bfloat16 [5, 128, 128], replicated, may hold values from -0.5 to 0.5
- fine_bias: float32 [128], replicated, may hold values from -3 to 3
- fine_gain: float32 [128], replicated, may hold values from 0.25 to 1.75
- coarse_weights: bfloat16 [2, 5, 128, 128], replicated, may hold values from -0.5 to 0.5
- coarse_bias: float32 [2, 128], replicated, may hold values from -3 to 3
- coarse_gain: float32 [2, 128], replicated, may hold values from 0.25 to 1.75
- cotangent: bfloat16 [4, 8, 512, 128], P('gx', 'gy'), may hold values from -6 to 6
Outputs:
- fine_out: bfloat16 [4, 8, 512, 128], P('gx', 'gy')
- grad_fine_weights: float32 [5, 128, 128], replicated
- grad_fine_bias: float32 [128], replicated
- grad_fine_gain: float32 [128], replicated
- grad_coarse_weights: float32 [2, 5, 128, 128], replicated
- grad_coarse_bias: float32 [2, 128], replicated
- grad_coarse_gain: float32 [2, 128], replicated
- grad_pooled: float32 [4, 8, 256, 128], P('gx', 'gy')
The draws below stay inside these ranges and needn't reach their ends.
Inputs may be any that keep to these rules, and one draw needn't show every extreme that they name: `fine_edges`: row 0 of each device's slots names senders: below 512 a node of the device, from 512 on a row of the four halo groups; row 1 names receivers among the device's 512 nodes. `fine_live`: A multiple of 512; in every draw some device has all 1536 slots live. `fine_halo`: block numbers of the device's fine nodes; within one device and direction they differ. `pool_map`: every coarse node of a device is named by at least one of its fine nodes. `coarse_edges`: row 0 names senders: below 256 a coarse node of the device, from 256 on a row of the four coarse halo groups; row 1 names receivers among the device's 256 coarse nodes. `coarse_halo`: block numbers of the device's coarse nodes.
All inputs are finite; a program needn't handle non-finite values.
Results may differ from the reference program's by a relative error of at most 0.009.
Values may be sent and summed in bfloat16 or wider, within the bound.
A program may use at most 64 MiB of HBM per device.

```python
import math
from functools import partial
import jax
import jax.numpy as jnp
from jax import lax

H = 128
BLOCK = 128
NF_DEV = 512
EDGE_BLOCK = 512
COARSE_STEPS = 2
EDGE_SLOTS = 1536
TURNS = 3
NC_DEV = 256
EC_DEV = 2048
FINE_HALO = 1
GRID_X = 4
GRID_Y = 8
FINE_NODES = 16384


def edge_draw(key, node_count, halo_count, slot_count):
    subkeys = jax.random.split(key, 4)
    grid_shape = (GRID_X, GRID_Y, slot_count)
    receivers = jax.random.randint(subkeys[0], grid_shape, 0, node_count)
    own_senders = jax.random.randint(subkeys[1], grid_shape, 0, node_count)
    remote = node_count + jax.random.randint(subkeys[2], grid_shape, 0, halo_count)
    senders = jnp.where(jax.random.randint(subkeys[3], grid_shape, 0, 4) == 0, remote, own_senders)
    return jnp.stack([senders, receivers], axis=2).astype(jnp.int32)


def distinct_blocks(key, block_count, chosen_count):
    scores = jax.random.randint(key, (GRID_X, GRID_Y, 4, block_count), 0, 1 << 20) * block_count + lax.iota(jnp.int32, block_count)
    ordered = jnp.argsort(scores, axis=-1, stable=True)
    return ordered[..., :chosen_count].astype(jnp.int32)


def draw_fine_edges(key, part):
    return edge_draw(jax.random.fold_in(key, 11), NF_DEV, 4 * FINE_HALO * BLOCK, EDGE_SLOTS)


def draw_coarse_edges(key, part):
    return edge_draw(jax.random.fold_in(key, 13), NC_DEV, 4 * BLOCK, EC_DEV)


def draw_fine_halo(key, part):
    return distinct_blocks(jax.random.fold_in(key, 15), NF_DEV // BLOCK, FINE_HALO)


def draw_coarse_halo(key, part):
    return distinct_blocks(jax.random.fold_in(key, 17), NC_DEV // BLOCK, 1)


def draw_pool_map(key, part):
    stride = NF_DEV // NC_DEV
    spots = lax.broadcasted_iota(jnp.int32, (GRID_X, GRID_Y, NF_DEV), 2)
    random_map = jax.random.randint(jax.random.fold_in(key, 19), (GRID_X, GRID_Y, NF_DEV), 0, NC_DEV)
    return jnp.where(spots % stride == 0, spots // stride, random_map).astype(jnp.int32)


def draw_fine_live(key, part):
    subkeys = jax.random.split(jax.random.fold_in(key, 21), 3)
    lowest = max(1, TURNS // 4)
    highest = max(lowest + 1, TURNS // 2 + 1)
    drawn = jax.random.randint(subkeys[0], (GRID_X, GRID_Y), lowest, highest)
    filled = jax.random.randint(subkeys[1], (GRID_X, GRID_Y), 0, 8) == 0
    chosen = jax.random.randint(subkeys[2], (), 0, GRID_X * GRID_Y)
    position = lax.broadcasted_iota(jnp.int32, (GRID_X, GRID_Y), 0) * GRID_Y + lax.broadcasted_iota(jnp.int32, (GRID_X, GRID_Y), 1)
    blocks = jnp.where(filled | (position == chosen), TURNS, drawn)
    return (blocks * EDGE_BLOCK).astype(jnp.int32)


def level_of(stream_key, dims, shards, least, largest):
    def one(dim, parts):
        heights = jax.random.uniform(jax.random.fold_in(jax.random.fold_in(stream_key, 6), dim), (parts,), jnp.float32, least / len(shards), largest / len(shards))
        return jnp.repeat(jnp.exp(heights), dims[dim] // parts).reshape((-1,) + (1,) * (len(dims) - dim - 1))

    factor_of = one(*shards[0])
    for cut in shards[1:]:
        factor_of = factor_of * one(*cut)
    return factor_of


def noise(stream_key, shape, scale, limit, cuts=(), held_as=jnp.bfloat16):
    level = level_of(stream_key, shape, cuts, -0.22, 0.18) if cuts else 1.0
    array = jax.random.normal(stream_key, shape, jnp.float32) * scale * level
    return jnp.minimum(jnp.maximum(array, -limit), limit).astype(held_as)


def setup_inputs(seed: int = 0) -> dict:
    key_list = jax.random.split(jax.random.key(seed), 15)
    return {
        "fine_nodes": noise(key_list[0], (GRID_X, GRID_Y, NF_DEV, H), 1.0, 6.0, ((0, 4), (1, 8))),
        "fine_edges": draw_fine_edges(jax.random.fold_in(key_list[14], 71), 0),
        "fine_live": draw_fine_live(jax.random.fold_in(key_list[14], 71), 0),
        "fine_halo": draw_fine_halo(jax.random.fold_in(key_list[14], 71), 0),
        "pool_map": draw_pool_map(jax.random.fold_in(key_list[14], 71), 0),
        "coarse_edges": draw_coarse_edges(jax.random.fold_in(key_list[14], 71), 0),
        "coarse_halo": draw_coarse_halo(jax.random.fold_in(key_list[14], 71), 0),
        "fine_weights": noise(key_list[7], (5, H, H), H ** -0.5, 0.5),
        "fine_bias": noise(key_list[8], (H,), 0.5, 3.0, (), jnp.float32),
        "fine_gain": jnp.clip(1.0 + 0.15 * jax.random.normal(key_list[9], (H,), jnp.float32), 0.25, 1.75),
        "coarse_weights": noise(key_list[10], (COARSE_STEPS, 5, H, H), H ** -0.5, 0.5),
        "coarse_bias": noise(key_list[11], (COARSE_STEPS, H), 0.5, 3.0, (), jnp.float32),
        "coarse_gain": jnp.clip(1.0 + 0.15 * jax.random.normal(key_list[12], (COARSE_STEPS, H), jnp.float32), 0.25, 1.75),
        "cotangent": noise(key_list[13], (GRID_X, GRID_Y, NF_DEV, H), 1.0, 6.0, ((0, 4), (1, 8))),
    }


EPSILON = 1e-05

def layer_norm(values):
    centred = values - lax.optimization_barrier(jnp.mean(values, axis=-1, keepdims=True))
    spread = lax.optimization_barrier(jnp.mean(centred * centred, axis=-1, keepdims=True))
    return centred * lax.rsqrt(spread + EPSILON)

def split_parts(values):
    high = values.astype(jnp.bfloat16)
    low = (values - high.astype(jnp.float32)).astype(jnp.bfloat16)
    return (high, low)

def contract_rows(left, right):
    high, low = split_parts(right)
    numbers = (((0,), (0,)), ((), ()))
    return lax.dot_general(left, high, numbers, preferred_element_type=jnp.float32) + lax.dot_general(left, low, numbers, preferred_element_type=jnp.float32)

def times_transpose(left, weight):
    high, low = split_parts(left)
    numbers = (((1,), (1,)), ((), ()))
    return lax.dot_general(high, weight, numbers, preferred_element_type=jnp.float32) + lax.dot_general(low, weight, numbers, preferred_element_type=jnp.float32)

def make_one_hot(pool_rows, coarse_count):
    return (pool_rows[:, None] == lax.iota(jnp.int32, coarse_count)[None, :]).astype(jnp.bfloat16)

def pick_blocks(node_rows, block_lists):
    features = node_rows.shape[-1]
    blocked = node_rows.reshape(-1, BLOCK, features)
    return blocked[block_lists].reshape(4, -1, features)

def put_blocks(returned, block_lists, row_count):
    features = returned.shape[-1]
    pieces = returned.reshape(-1, BLOCK, features)
    total = jnp.zeros((row_count // BLOCK, BLOCK, features), jnp.float32).at[block_lists.reshape(-1)].add(pieces)
    return total.reshape(row_count, features)

def slot_block(edge_list, live_slots, first_slot, block_width):
    senders = lax.dynamic_slice_in_dim(edge_list[0], first_slot, block_width)
    receivers = lax.dynamic_slice_in_dim(edge_list[1], first_slot, block_width)
    weights_live = (first_slot + lax.iota(jnp.int32, block_width) < live_slots).astype(jnp.float32)
    return (senders, receivers, weights_live)

def step_forward(node_rows, halo_rows, edge_list, live_slots, turn_count, weights, edge_bias, norm_gain, block_width):
    row_count = node_rows.shape[0]
    extended = jnp.concatenate([node_rows, halo_rows], axis=0)
    proj_send = jnp.dot(extended, weights[0], preferred_element_type=jnp.float32)
    proj_recv = jnp.dot(node_rows, weights[1], preferred_element_type=jnp.float32)

    def one_turn(turn_index, running):
        first_slot = (turn_index * block_width).astype(jnp.int32)
        senders, receivers, weights_live = slot_block(edge_list, live_slots, first_slot, block_width)
        hidden = jax.nn.silu(proj_send[senders] + proj_recv[receivers] + edge_bias).astype(jnp.bfloat16)
        message = jnp.dot(hidden, weights[2], preferred_element_type=jnp.float32) * weights_live[:, None]
        return running.at[receivers].add(message)
    summed = lax.fori_loop(0, turn_count, one_turn, jnp.zeros((row_count, proj_recv.shape[1]), jnp.float32))
    agg_low = summed.astype(jnp.bfloat16)
    node_pre = jnp.dot(node_rows, weights[3], preferred_element_type=jnp.float32) + jnp.dot(agg_low, weights[4], preferred_element_type=jnp.float32)
    output = (node_rows.astype(jnp.float32) + norm_gain * layer_norm(node_pre)).astype(jnp.bfloat16)
    return (output, (extended, proj_send, proj_recv, agg_low, node_pre))

def step_backward(upstream, node_rows, saved_state, edge_list, live_slots, turn_count, weights, edge_bias, norm_gain, block_width, want_input):
    extended, proj_send, proj_recv, agg_low, node_pre = saved_state
    row_count = node_rows.shape[0]
    features = proj_recv.shape[1]
    normed, norm_back = jax.vjp(layer_norm, node_pre)
    grad_gain = lax.optimization_barrier(jnp.sum(upstream * normed, axis=0))
    grad_pre = norm_back(upstream * norm_gain)[0]
    grad_self = contract_rows(node_rows, grad_pre)
    grad_agg_weight = contract_rows(agg_low, grad_pre)
    grad_agg = times_transpose(grad_pre, weights[4])

    def one_turn(turn_index, running):
        grad_send, grad_recv, grad_bias, grad_msg = running
        first_slot = (turn_index * block_width).astype(jnp.int32)
        senders, receivers, weights_live = slot_block(edge_list, live_slots, first_slot, block_width)
        pre_act = proj_send[senders] + proj_recv[receivers] + edge_bias
        hidden = jax.nn.silu(pre_act).astype(jnp.bfloat16)
        grad_message = grad_agg[receivers] * weights_live[:, None]
        grad_msg = grad_msg + contract_rows(hidden, grad_message)
        sigmoid = jax.nn.sigmoid(pre_act)
        grad_act = times_transpose(grad_message, weights[2]) * sigmoid * (1.0 + pre_act * (1.0 - sigmoid))
        return (grad_send.at[senders].add(grad_act), grad_recv.at[receivers].add(grad_act), grad_bias + lax.optimization_barrier(jnp.sum(grad_act, axis=0)), grad_msg)
    start_state = (jnp.zeros(proj_send.shape, jnp.float32), jnp.zeros(proj_recv.shape, jnp.float32), jnp.zeros((features,), jnp.float32), jnp.zeros((features, features), jnp.float32))
    grad_send, grad_recv, grad_bias, grad_msg = lax.fori_loop(0, turn_count, one_turn, start_state)
    grad_weights = jnp.stack([contract_rows(extended, grad_send), contract_rows(node_rows, grad_recv), grad_msg, grad_self, grad_agg_weight])
    if not want_input:
        return ((grad_weights, grad_bias, grad_gain), None, None)
    grad_ext = times_transpose(grad_send, weights[0])
    grad_nodes = upstream + times_transpose(grad_pre, weights[3]) + times_transpose(grad_recv, weights[1]) + grad_ext[:row_count]
    return ((grad_weights, grad_bias, grad_gain), grad_nodes, grad_ext[row_count:])

def from_lower(values, axis):
    length = values.shape[axis]
    zero_part = jnp.zeros_like(lax.slice_in_dim(values, 0, 1, axis=axis))
    return jnp.concatenate([zero_part, lax.slice_in_dim(values, 0, length - 1, axis=axis)], axis=axis)

def from_upper(values, axis):
    length = values.shape[axis]
    zero_part = jnp.zeros_like(lax.slice_in_dim(values, 0, 1, axis=axis))
    return jnp.concatenate([lax.slice_in_dim(values, 1, length, axis=axis), zero_part], axis=axis)

def assemble(grid_rows, block_lists):
    sends = jax.vmap(jax.vmap(pick_blocks))(grid_rows, block_lists)
    groups = [from_lower(sends[:, :, 1], 0), from_upper(sends[:, :, 0], 0), from_lower(sends[:, :, 3], 1), from_upper(sends[:, :, 2], 1)]
    return jnp.concatenate(groups, axis=2)

def assemble_back(halo_grads, block_lists, row_count):
    split = halo_grads.reshape(halo_grads.shape[:2] + (4, -1, halo_grads.shape[-1]))
    returned = jnp.stack([from_lower(split[:, :, 1], 0), from_upper(split[:, :, 0], 0), from_lower(split[:, :, 3], 1), from_upper(split[:, :, 2], 1)], axis=2)
    return jax.vmap(jax.vmap(partial(put_blocks, row_count=row_count)))(returned, block_lists)

def sum_devices(values):
    return lax.optimization_barrier(jnp.sum(values, axis=0))

def reference(fine_nodes, fine_edges, fine_live, fine_halo, pool_map, coarse_edges, coarse_halo, fine_weights, fine_bias, fine_gain, coarse_weights, coarse_bias, coarse_gain, cotangent):
    device_count = GRID_X * GRID_Y
    fine_turns = EDGE_SLOTS // EDGE_BLOCK
    coarse_slots = EC_DEV
    coarse_turns = EC_DEV // EDGE_BLOCK
    loss_scale = 1.0 / math.sqrt(FINE_NODES)

    def flatten(values):
        return values.reshape((device_count,) + values.shape[2:])

    def gridded(values):
        return values.reshape((GRID_X, GRID_Y) + values.shape[1:])
    fine_ext = flatten(assemble(fine_nodes, fine_halo))
    flat_nodes = flatten(fine_nodes)
    flat_edges = flatten(fine_edges)
    flat_live = flatten(fine_live)
    flat_pool = flatten(pool_map)
    flat_coarse_edges = flatten(coarse_edges)
    flat_cot = flatten(cotangent)

    def fine_ahead(device_item):
        node_rows, halo_rows, edge_list, live_slots = device_item
        return step_forward(node_rows, halo_rows, edge_list, live_slots, fine_turns, fine_weights, fine_bias, fine_gain, EDGE_BLOCK)[0]
    fine_mid = lax.map(fine_ahead, (flat_nodes, fine_ext, flat_edges, flat_live))

    def pooling(device_item):
        mid_rows, pool_rows = device_item
        one_hot = make_one_hot(pool_rows, NC_DEV)
        pooled_sums = lax.dot_general(one_hot, mid_rows, (((0,), (0,)), ((), ())), preferred_element_type=jnp.float32)
        counts = lax.optimization_barrier(jnp.sum(one_hot, axis=0, dtype=jnp.float32))
        return ((pooled_sums / counts[:, None]).astype(jnp.bfloat16), counts)
    current, counts = lax.map(pooling, (fine_mid, flat_pool))

    def coarse_ahead(step_index, device_item):
        node_rows, halo_rows, edge_list = device_item
        return step_forward(node_rows, halo_rows, edge_list, coarse_slots, coarse_turns, coarse_weights[step_index], coarse_bias[step_index], coarse_gain[step_index], EDGE_BLOCK)[0]
    states = []
    for step_index in range(COARSE_STEPS):
        ext_now = flatten(assemble(gridded(current), coarse_halo))
        states.append((current, ext_now))
        current = lax.map(partial(coarse_ahead, step_index), (current, ext_now, flat_coarse_edges))

    def unpooling(device_item):
        mid_rows, pool_rows, coarse_rows = device_item
        lifted = jnp.dot(make_one_hot(pool_rows, NC_DEV), coarse_rows, preferred_element_type=jnp.float32)
        return (mid_rows.astype(jnp.float32) + lifted).astype(jnp.bfloat16)
    fine_out = lax.map(unpooling, (fine_mid, flat_pool, current))

    def coarse_seed(device_item):
        cot_rows, pool_rows = device_item
        return jax.ops.segment_sum(cot_rows.astype(jnp.float32) * loss_scale, pool_rows, num_segments=NC_DEV)
    upstream = lax.map(coarse_seed, (flat_cot, flat_pool))

    def coarse_behind(step_index, device_item):
        grad_rows, node_rows, halo_rows, edge_list = device_item
        saved_state = step_forward(node_rows, halo_rows, edge_list, coarse_slots, coarse_turns, coarse_weights[step_index], coarse_bias[step_index], coarse_gain[step_index], EDGE_BLOCK)[1]
        return step_backward(grad_rows, node_rows, saved_state, edge_list, coarse_slots, coarse_turns, coarse_weights[step_index], coarse_bias[step_index], coarse_gain[step_index], EDGE_BLOCK, True)
    coarse_terms = [None] * COARSE_STEPS
    for step_index in reversed(range(COARSE_STEPS)):
        inputs_now, ext_now = states[step_index]
        step_terms, grad_nodes, grad_halo = lax.map(partial(coarse_behind, step_index), (upstream, inputs_now, ext_now, flat_coarse_edges))
        upstream = grad_nodes + flatten(assemble_back(gridded(grad_halo), coarse_halo, NC_DEV))
        coarse_terms[step_index] = jax.tree.map(sum_devices, step_terms)
    grad_pooled = gridded(upstream * math.sqrt(FINE_NODES))

    def fine_behind(device_item):
        node_rows, halo_rows, edge_list, live_slots, cot_rows, pool_rows, coarse_up, coarse_counts = device_item
        saved_state = step_forward(node_rows, halo_rows, edge_list, live_slots, fine_turns, fine_weights, fine_bias, fine_gain, EDGE_BLOCK)[1]
        direct = cot_rows.astype(jnp.float32) * loss_scale
        fine_seed = direct + (coarse_up / coarse_counts[:, None])[pool_rows]
        return step_backward(fine_seed, node_rows, saved_state, edge_list, live_slots, fine_turns, fine_weights, fine_bias, fine_gain, EDGE_BLOCK, False)[0]
    fine_terms = jax.tree.map(sum_devices, lax.map(fine_behind, (flat_nodes, fine_ext, flat_edges, flat_live, flat_cot, flat_pool, upstream, counts)))
    grad_coarse_weights = jnp.stack([entry[0] for entry in coarse_terms])
    grad_coarse_bias = jnp.stack([entry[1] for entry in coarse_terms])
    grad_coarse_gain = jnp.stack([entry[2] for entry in coarse_terms])
    return (gridded(fine_out), fine_terms[0], fine_terms[1], fine_terms[2], grad_coarse_weights, grad_coarse_bias, grad_coarse_gain, grad_pooled)
```

```python
import functools
import math

import jax
import jax.numpy as jnp
from jax import lax
from jax.experimental import pallas as pl
from jax.experimental.pallas import tpu as pltpu
from jax.sharding import PartitionSpec as P

BLOCK = 128
NC_DEV = 256
LANES = 128
EPSILON = 1e-05
MESH = pl.DeviceIdType.MESH
BF = jnp.bfloat16
F32 = jnp.float32
ROWS = 512


def dot(a, b):
    return lax.dot_general(a, b, (((1,), (0,)), ((), ())), preferred_element_type=F32)


def dot_t(a, b):
    return lax.dot_general(a, b, (((1,), (1,)), ((), ())), preferred_element_type=F32)


def dot_rows(a, b):
    return lax.dot_general(a, b, (((0,), (0,)), ((), ())), preferred_element_type=F32)


def parts(values):
    high = values.astype(BF)
    low = (values - high.astype(F32)).astype(BF)
    return high, low


def side(*pieces):
    return jnp.concatenate(pieces, axis=1)


def halves(values):
    width = values.shape[1] // 2
    return values[:, :width] + values[:, width:]


def times_t(left, weight):
    return dot_t(side(*parts(left)), side(weight, weight))


def norm(values):
    centred = values - jnp.mean(values, axis=-1, keepdims=True)
    spread = jnp.mean(centred * centred, axis=-1, keepdims=True)
    scale = lax.rsqrt(spread + EPSILON)
    return centred * scale, scale


def norm_back(grad, normed, scale):
    first = jnp.mean(grad, axis=-1, keepdims=True)
    second = jnp.mean(grad * normed, axis=-1, keepdims=True)
    return scale * (grad - first - normed * second)


def round_up(value, step):
    return (value + step - 1) // step * step


def marks(offsets, start):
    return jnp.where(offsets == start, 1.0, 0.0).astype(BF)


def step_kernel(nx, ny, loss_scale, out_scale, group_rows, fnodes, fedges, flive, fhalo_list, pool, cedges, chalo_list,
                fw, fb, fg, cw, cb, cg, cot, fine_out, grad_out, pooled_out,
                f_ps, f_pr, f_prt, c_ps, c_pr, c_pt, p_p, p_t, halo_in, halo_out, f_x, c_x, hid, slope_f, slope_c, g_hl,
                f_high, f_agg, f_norm, f_scale, c_cur, c_high, c_agg, c_norm, c_scale, f_mid, counts, ups, work,
                sb0, sb1, sb2, sb3, ra0, ra1, ra2, ra3, rb0, rb1, rb2, rb3, rc0, rc1, rc2, rc3,
                halo_send, halo_recv, rs_send, rs_recv, ex_send, ex_recv, ag_send, ag_recv):
    sb, ra, rb, rc = (sb0, sb1, sb2, sb3), (ra0, ra1, ra2, ra3), (rb0, rb1, rb2, rb3), (rc0, rc1, rc2, rc3)
    gx, gy = lax.axis_index("gx"), lax.axis_index("gy")
    nf, ef = fnodes.shape[2], fedges.shape[3]
    nc, ec = c_cur.shape[1], cedges.shape[3]
    width = halo_in.shape[2]
    span = 4 * width
    x_peers = [lax.rem(gx + d, nx) for d in range(1, nx)]
    y_peers = [lax.rem(gy + d, ny) for d in range(1, ny)]

    barrier = pltpu.get_barrier_semaphore()
    for peer in x_peers:
        pl.semaphore_signal(barrier, inc=1, device_id=(peer, gy), device_id_type=MESH)
    for peer in y_peers:
        pl.semaphore_signal(barrier, inc=1, device_id=(gx, peer), device_id_type=MESH)

    lane = lax.broadcasted_iota(jnp.int32, (LANES, LANES), 1)
    sub = lax.broadcasted_iota(jnp.int32, (LANES, LANES), 0)

    def edge_row(edges, row, start, live):
        picked = edges[0, 0, pl.ds(row, 1), pl.ds(start, LANES)]
        wide = jnp.broadcast_to(picked, (LANES, LANES))
        if live is not None:
            wide = jnp.where(lane + start < live, wide, -1)
        return wide

    def mark_rows(dst, wide, start, count):
        offsets = wide.T - lane
        for c in range(count // LANES):
            dst[pl.ds(start, LANES), pl.ds(c * LANES, LANES)] = marks(offsets, c * LANES)

    def mark_cols(dst, base, wide, start, count):
        offsets = wide - sub
        for c in range(count // LANES):
            dst[pl.ds(base + c * LANES, LANES), pl.ds(start, LANES)] = marks(offsets, c * LANES)

    has = (gx > 0, gx < nx - 1, gy > 0, gy < ny - 1)
    place = ((gx - 1, gy), (gx + 1, gy), (gx, gy - 1), (gx, gy + 1))
    far = (1, 0, 3, 2)

    def halo_copy(turn, d):
        return pltpu.make_async_remote_copy(
            src_ref=halo_out.at[turn, d], dst_ref=halo_in.at[turn, pl.ds(far[d] * width, width)],
            send_sem=halo_send.at[turn, d], recv_sem=halo_recv.at[turn, far[d]],
            device_id=place[d], device_id_type=MESH)

    def halo_start(turn):
        for d in range(4):
            @pl.when(has[d])
            def _(d=d):
                halo_copy(turn, d).start()

    def halo_wait(turn):
        for d in range(4):
            @pl.when(has[d])
            def _(d=d):
                pltpu.make_async_remote_copy(
                    src_ref=halo_out.at[turn, d], dst_ref=halo_in.at[turn, pl.ds(d * width, width)],
                    send_sem=halo_send.at[turn, d], recv_sem=halo_recv.at[turn, d],
                    device_id=place[d], device_id_type=MESH).wait_recv()

    def halo_flush(turn):
        for d in range(4):
            @pl.when(has[d])
            def _(d=d):
                halo_copy(turn, d).wait_send()

    def is_block(target, b):
        return jnp.where(target == b, 1.0, 0.0)

    def pick_block(turn, d, m, target, blocks):
        total = blocks[0].astype(F32) * is_block(target, 0)
        for b in range(1, len(blocks)):
            total = total + blocks[b].astype(F32) * is_block(target, b)
        halo_out[turn, d, m * BLOCK:(m + 1) * BLOCK, :] = total.astype(BF)

    chunk = [rows // nx for rows in group_rows]

    def rs_copies(g):
        return [pltpu.make_async_remote_copy(
            src_ref=sb[g].at[pl.ds(pl.multiple_of(peer * chunk[g], 16), chunk[g])], dst_ref=ra[g].at[d],
            send_sem=rs_send.at[g, d], recv_sem=rs_recv.at[g, d],
            device_id=(peer, gy), device_id_type=MESH) for d, peer in enumerate(x_peers)]

    def ex_copies(g):
        return [pltpu.make_async_remote_copy(
            src_ref=rb[g].at[gy], dst_ref=rb[g].at[gy], send_sem=ex_send.at[g, d], recv_sem=ex_recv.at[g, d],
            device_id=(gx, peer), device_id_type=MESH) for d, peer in enumerate(y_peers)]

    def ag_copies(g):
        return [pltpu.make_async_remote_copy(
            src_ref=rc[g].at[gx], dst_ref=rc[g].at[gx], send_sem=ag_send.at[g, d], recv_sem=ag_recv.at[g, d],
            device_id=(peer, gy), device_id_type=MESH) for d, peer in enumerate(x_peers)]

    def put_terms(g, blocks, vectors):
        rows = 0
        for block in blocks:
            sb[g][rows:rows + LANES, :] = block.astype(BF)
            rows += LANES
        rest = group_rows[g] - rows
        lines = jnp.concatenate(vectors + [jnp.zeros((16 - len(vectors), LANES), F32)], axis=0)
        sb[g][rows:rows + 16, :] = lines.astype(BF)
        if rest > 16:
            sb[g][rows + 16:, :] = jnp.zeros((rest - 16, LANES), BF)

    def sum_first(g):
        for copy in rs_copies(g):
            copy.start()

    def sum_second(g):
        for copy in rs_copies(g):
            copy.wait_recv()
        total = sb[g][pl.ds(pl.multiple_of(gx * chunk[g], 16), chunk[g]), :].astype(F32)
        for d in range(nx - 1):
            total = total + ra[g][d].astype(F32)
        rb[g][gy] = total.astype(BF)
        for copy in ex_copies(g):
            copy.start()

    def sum_third(g):
        for copy in ex_copies(g):
            copy.wait_recv()
        total = rb[g][0].astype(F32)
        for j in range(1, ny):
            total = total + rb[g][j].astype(F32)
        rc[g][gx] = total.astype(BF)
        for copy in ag_copies(g):
            copy.start()

    def sum_fourth(g, start):
        for copy in ag_copies(g):
            copy.wait_recv()
        for i in range(nx):
            grad_out[start + i * chunk[g]:start + (i + 1) * chunk[g], :] = rc[g][i]

    def sum_flush(g):
        for copy in rs_copies(g) + ex_copies(g) + ag_copies(g):
            copy.wait_send()

    live = flive[0, 0]
    for d in range(4):
        for m in range(width // BLOCK):
            pick_block(0, d, m, fhalo_list[0, 0, d, m], [fnodes[0, 0, n:n + BLOCK, :] for n in range(0, nf, BLOCK)])
    for turn in range(5):
        for d in range(4):
            @pl.when(jnp.logical_not(has[d]))
            def _(turn=turn, d=d):
                halo_in[turn, pl.ds(d * width, width), :] = jnp.zeros((width, LANES), BF)

    pl.semaphore_wait(barrier, nx + ny - 2)
    halo_start(0)

    @pl.loop(0, ef // LANES)
    def _(i):
        start = pl.multiple_of(i * LANES, LANES)
        senders = edge_row(fedges, 0, start, live)
        receivers = edge_row(fedges, 1, start, live)
        mark_rows(f_ps, senders, start, nf + span)
        mark_rows(f_pr, receivers, start, nf)
        mark_cols(f_prt, 0, receivers, start, nf)

    @pl.loop(0, nf // LANES)
    def _(i):
        start = pl.multiple_of(i * LANES, LANES)
        picked = pool[0, 0:1, pl.ds(start, LANES)]
        wide = jnp.broadcast_to(picked[0:1], (LANES, LANES))
        mark_rows(p_p, wide, start, nc)
        mark_cols(p_t, 0, wide, start, nc)

    seed = dot(p_t[...], side(cot[0, 0], jnp.ones((nf, LANES), BF)))
    ups[...] = seed[:, :LANES] * loss_scale
    counts[...] = seed[:, LANES:]

    def pick_own(ps, pr, x, rows_of, count, edges):
        @pl.loop(0, edges // ROWS)
        def _(i):
            rows = pl.ds(pl.multiple_of(i * ROWS, ROWS), ROWS)
            own = rows_of()
            x[rows, 0:LANES] = dot(ps[rows, 0:count], own).astype(BF)
            x[rows, LANES:2 * LANES] = dot(pr[rows, :], own).astype(BF)

    def activate(ps, x, halo, count, w01, bias, slope, edges):
        @pl.loop(0, edges // ROWS)
        def _(i):
            rows = pl.ds(pl.multiple_of(i * ROWS, ROWS), ROWS)
            more = dot(ps[rows, count:count + span], halo())
            both = side((x[rows, 0:LANES].astype(F32) + more).astype(BF), x[rows, LANES:2 * LANES])
            x[rows, 0:LANES] = both[:, :LANES]
            pre = dot(both, w01) + bias
            gate = jax.nn.sigmoid(pre)
            hid[rows, :] = (pre * gate).astype(BF)
            slope[rows, :] = gate * (1.0 + pre * (1.0 - gate))

    def weight(w, k):
        return w[k]

    def pair(w, k):
        return jnp.concatenate([weight(w, k), weight(w, k + 1)], axis=0)

    def settle(rows_of, prt, high_ref, agg_ref, norm_ref, scale_ref, w, gain, edges):
        high, low = parts(dot(prt, hid[0:edges, :]))
        w2 = weight(w, 2)
        agg = dot(side(high, low), jnp.concatenate([w2, w2], axis=0)).astype(BF)
        own = rows_of()
        normed, scale = norm(dot(side(own, agg), pair(w, 3)))
        high_ref[...] = high
        agg_ref[...] = agg
        norm_ref[...] = normed
        scale_ref[...] = jnp.broadcast_to(scale, normed.shape)
        return (own.astype(F32) + gain * normed).astype(BF)

    def fine_rows():
        return fnodes[0, 0]

    pick_own(f_ps, f_pr, f_x, fine_rows, nf, ef)
    halo_wait(0)
    activate(f_ps, f_x, lambda: halo_in[0], nf, pair(fw, 0), fb[...][None, :], slope_f, ef)
    mid = settle(fine_rows, f_prt[...], f_high, f_agg, f_norm, f_scale, fw, fg[...][None, :], ef)
    f_mid[...] = mid

    c_cur[0] = (dot(p_t[...], mid) / counts[...]).astype(BF)

    def coarse_send(k):
        for d in range(4):
            for m in range(width // BLOCK):
                pick_block(1 + k, d, m, chalo_list[0, 0, d, m], [c_cur[k, n:n + BLOCK, :] for n in range(0, nc, BLOCK)])
        halo_start(1 + k)

    coarse_send(0)

    @pl.loop(0, ec // LANES)
    def _(i):
        start = pl.multiple_of(i * LANES, LANES)
        senders = edge_row(cedges, 0, start, None)
        receivers = edge_row(cedges, 1, start, None)
        mark_rows(c_ps, senders, start, nc + span)
        mark_rows(c_pr, receivers, start, nc)
        mark_cols(c_pt, 0, senders, start, nc + span)
        mark_cols(c_pt, nc + span, receivers, start, nc)

    steps = cw.shape[0]
    for k in range(steps):
        def rows_of(k=k):
            return c_cur[k]

        pick_own(c_ps, c_pr, c_x, rows_of, nc, ec)
        halo_wait(1 + k)
        activate(c_ps, c_x, lambda k=k: halo_in[1 + k], nc, pair(cw.at[k], 0), cb[k:k + 1, :], slope_c.at[k], ec)
        after = settle(rows_of, c_pt[nc + span:, :], c_high.at[k], c_agg.at[k], c_norm.at[k], c_scale.at[k], cw.at[k],
                       cg[k:k + 1, :], ec)
        c_cur[k + 1] = after
        if k + 1 < steps:
            coarse_send(k + 1)

    def back_nodes(up, norm_ref, scale_ref, w, gain):
        normed = norm_ref[...]
        grad_gain = jnp.sum(up * normed, axis=0, keepdims=True)
        grad_pre = norm_back(up * gain, normed, scale_ref[...])
        grad_agg = times_t(grad_pre, weight(w, 4))
        grad_hidden = times_t(grad_agg, weight(w, 2))
        return grad_gain, grad_pre, grad_agg, side(*parts(grad_hidden))

    def back_edges(pr, hidden_parts, slope, edges):
        work[0:hidden_parts.shape[0], :] = hidden_parts
        count = hidden_parts.shape[0]

        def one(i, total):
            rows = pl.ds(pl.multiple_of(i * ROWS, ROWS), ROWS)
            grad = halves(dot(pr[rows, :], work[0:count, :])) * slope[rows, :]
            g_hl[rows, :] = side(*parts(grad))
            return total + jnp.sum(grad.reshape(ROWS // 8, 8, LANES), axis=0)

        return jnp.sum(lax.fori_loop(0, edges // ROWS, one, jnp.zeros((8, LANES), F32)), axis=0, keepdims=True)

    def node_terms(own, agg, high, grad_pre, grad_agg):
        last = halves_of(dot_rows(side(own, agg), side(*parts(grad_pre))))
        message = halves(dot_rows(high, side(*parts(grad_agg))))
        return message, last[:LANES], last[LANES:]

    def halves_of(values):
        return values[:, :LANES] + values[:, LANES:]

    c_groups = [None] * steps
    for k in reversed(range(steps)):
        turn = 3 + (steps - 1 - k)
        g = steps - 1 - k
        w = cw.at[k]
        up = ups[...]
        grad_gain, grad_pre, grad_agg, hidden_parts = back_nodes(up, c_norm.at[k], c_scale.at[k], w, cg[k:k + 1, :])
        grad_bias = back_edges(c_pr, hidden_parts, slope_c.at[k], ec)
        far_send = halves(dot(c_pt[nc:nc + span, :], g_hl[...]))
        far_grad = times_t(far_send, weight(w, 0)).astype(BF)
        for d in range(4):
            halo_out[turn, d] = far_grad[d * width:(d + 1) * width]
        halo_start(turn)
        own_send = halves(dot(c_pt[0:nc, :], g_hl[...]))
        own_recv = halves(dot(c_pt[nc + span:, :], g_hl[...]))
        own = c_cur[k]
        nodes_grad = up + dot_t(
            side(*parts(grad_pre), *parts(own_recv), *parts(own_send)),
            side(weight(w, 3), weight(w, 3), weight(w, 1), weight(w, 1), weight(w, 0), weight(w, 0)))
        sender = halves(dot_rows(own, side(*parts(own_send)))) + halves(dot_rows(halo_in[1 + k], side(*parts(far_send))))
        receiver = halves(dot_rows(own, side(*parts(own_recv))))
        message, self_term, agg_term = node_terms(own, c_agg[k], c_high[k], grad_pre, grad_agg)
        put_terms(g, [sender, receiver, message, self_term, agg_term], [grad_bias, grad_gain])
        sum_first(g)
        if g == 0:
            lifted = dot(p_p[...], c_cur[steps])
            fine_out[...] = (f_mid[...].astype(F32) + lifted).astype(BF)
        else:
            sum_second(g - 1)
        halo_wait(turn)
        blocks = [nodes_grad[b * BLOCK:(b + 1) * BLOCK] for b in range(nc // BLOCK)]
        for d in range(4):
            for m in range(width // BLOCK):
                target = chalo_list[0, 0, d, m]
                back = halo_in[turn, pl.ds(d * width + m * BLOCK, BLOCK), :].astype(F32)
                blocks = [block + back * is_block(target, b) for b, block in enumerate(blocks)]
        ups[...] = jnp.concatenate(blocks, axis=0)

    up = ups[...]
    pooled_out[...] = up * out_scale
    spread = up / counts[...]
    fine_up = cot[0, 0].astype(F32) * loss_scale + halves(dot(p_p[...], side(*parts(spread))))
    grad_gain, grad_pre, grad_agg, hidden_parts = back_nodes(fine_up, f_norm, f_scale, fw, fg[...][None, :])
    message, self_term, agg_term = node_terms(fine_rows(), f_agg[...], f_high[...], grad_pre, grad_agg)
    put_terms(2, [message, self_term, agg_term], [grad_gain])
    sum_first(2)
    grad_bias = back_edges(f_pr, hidden_parts, slope_f, ef)
    ends = halves_of(dot_rows(f_x[...], g_hl[0:ef, :]))
    put_terms(3, [ends[:LANES], ends[LANES:]], [grad_bias])
    sum_first(3)
    sum_third(0)
    sum_second(1)
    sum_second(2)
    sum_second(3)
    starts = [sum(group_rows[:g]) for g in range(4)]
    sum_third(1)
    sum_third(2)
    sum_third(3)
    for g in range(4):
        sum_fourth(g, starts[g])
    for turn in range(5):
        halo_flush(turn)
    for g in range(4):
        sum_flush(g)


def finish_kernel(group_rows, fine_in, grads, pooled_in, fine_out, gfw, gfb, gfg, gcw, gcb, gcg, pooled_out):
    fine_out[0, 0] = fine_in[...]
    pooled_out[0, 0] = pooled_in[...]
    starts = [sum(group_rows[:g]) for g in range(4)]

    def block(start):
        return grads[start:start + LANES, :].astype(F32)

    def lines(start):
        return grads[start:start + 16, :].astype(F32)

    steps = gcw.shape[0]
    for k in range(steps):
        start = starts[steps - 1 - k]
        for n in range(5):
            gcw[k, n] = block(start + n * LANES)
        tail = lines(start + 5 * LANES)
        gcb[k:k + 1, :] = tail[0:1]
        gcg[k:k + 1, :] = tail[1:2]
    for n in range(2):
        gfw[n] = block(starts[3] + n * LANES)
    for n in range(3):
        gfw[2 + n] = block(starts[2] + n * LANES)
    gfb[...] = lines(starts[3] + 2 * LANES)[0]
    gfg[...] = lines(starts[2] + 3 * LANES)[0]


def body(nx, ny, fine_nodes, fine_edges, fine_live, fine_halo, pool_map, coarse_edges, coarse_halo,
         fine_weights, fine_bias, fine_gain, coarse_weights, coarse_bias, coarse_gain, cotangent):
    nf, h = fine_nodes.shape[2:]
    ef, ec = fine_edges.shape[3], coarse_edges.shape[3]
    nc = NC_DEV
    steps = coarse_weights.shape[0]
    fw_span = 4 * fine_halo.shape[3] * BLOCK
    cw_span = 4 * coarse_halo.shape[3] * BLOCK
    width = fw_span // 4
    assert fw_span == cw_span and h == LANES and steps == 2
    loss_scale = 1.0 / math.sqrt(nf * nx * ny)
    out_scale = math.sqrt(nf * nx * ny)
    unit = nx * 16
    group_rows = tuple(round_up(r + 16, unit) for r in (5 * h, 5 * h, 3 * h, 2 * h))
    vmem = pl.BlockSpec(memory_space=pltpu.VMEM)
    smem = pl.BlockSpec(memory_space=pltpu.SMEM)
    scratch = [
        pltpu.VMEM((ef, nf + fw_span), BF), pltpu.VMEM((ef, nf), BF), pltpu.VMEM((nf, ef), BF),
        pltpu.VMEM((ec, nc + cw_span), BF), pltpu.VMEM((ec, nc), BF), pltpu.VMEM((nc + cw_span + nc, ec), BF),
        pltpu.VMEM((nf, nc), BF), pltpu.VMEM((nc, nf), BF),
        pltpu.VMEM((5, 4 * width, h), BF), pltpu.VMEM((5, 4, width, h), BF),
        pltpu.VMEM((ef, 2 * h), BF), pltpu.VMEM((ec, 2 * h), BF), pltpu.VMEM((max(ef, ec), h), BF),
        pltpu.VMEM((ef, h), F32), pltpu.VMEM((steps, ec, h), F32), pltpu.VMEM((max(ef, ec), 2 * h), BF),
        pltpu.VMEM((nf, h), BF), pltpu.VMEM((nf, h), BF), pltpu.VMEM((nf, h), F32), pltpu.VMEM((nf, h), F32),
        pltpu.VMEM((steps + 1, nc, h), BF), pltpu.VMEM((steps, nc, h), BF), pltpu.VMEM((steps, nc, h), BF),
        pltpu.VMEM((steps, nc, h), F32), pltpu.VMEM((steps, nc, h), F32),
        pltpu.VMEM((nf, h), BF), pltpu.VMEM((nc, h), F32), pltpu.VMEM((nc, h), F32), pltpu.VMEM((max(nf, nc), 2 * h), BF),
    ]
    scratch += [pltpu.VMEM((r, h), BF) for r in group_rows]
    scratch += [pltpu.VMEM((nx - 1, r // nx, h), BF) for r in group_rows]
    scratch += [pltpu.VMEM((ny, r // nx, h), BF) for r in group_rows]
    scratch += [pltpu.VMEM((nx, r // nx, h), BF) for r in group_rows]
    dma = pltpu.SemaphoreType.DMA
    scratch += [dma((5, 4)), dma((5, 4)), dma((4, nx - 1)), dma((4, nx - 1)), dma((4, ny - 1)), dma((4, ny - 1)),
                dma((4, nx - 1)), dma((4, nx - 1))]
    fine_mid, grads, pooled = pl.pallas_call(
        functools.partial(step_kernel, nx, ny, loss_scale, out_scale, group_rows),
        out_shape=(jax.ShapeDtypeStruct((nf, h), BF), jax.ShapeDtypeStruct((sum(group_rows), h), BF),
                   jax.ShapeDtypeStruct((nc, h), F32)),
        in_specs=[vmem, vmem, smem, smem, vmem, vmem, smem, vmem, vmem, vmem, vmem, vmem, vmem, vmem],
        out_specs=(vmem, vmem, vmem),
        scratch_shapes=scratch,
        compiler_params=pltpu.CompilerParams(collective_id=0, has_side_effects=True, vmem_limit_bytes=48 * 1024 * 1024),
        name="step",
    )(fine_nodes, fine_edges, fine_live, fine_halo, pool_map, coarse_edges, coarse_halo,
      fine_weights, fine_bias, fine_gain, coarse_weights, coarse_bias, coarse_gain, cotangent)
    return pl.pallas_call(
        functools.partial(finish_kernel, group_rows),
        out_shape=(jax.ShapeDtypeStruct((1, 1, nf, h), BF), jax.ShapeDtypeStruct(fine_weights.shape, F32),
                   jax.ShapeDtypeStruct(fine_bias.shape, F32), jax.ShapeDtypeStruct(fine_gain.shape, F32),
                   jax.ShapeDtypeStruct(coarse_weights.shape, F32), jax.ShapeDtypeStruct(coarse_bias.shape, F32),
                   jax.ShapeDtypeStruct(coarse_gain.shape, F32), jax.ShapeDtypeStruct((1, 1, nc, h), F32)),
        in_specs=[vmem] * 3,
        out_specs=(vmem,) * 8,
        name="finish",
    )(fine_mid, grads, pooled)


def solution(mesh):
    grid = P("gx", "gy")
    return jax.shard_map(
        functools.partial(body, mesh.shape["gx"], mesh.shape["gy"]),
        mesh=mesh,
        in_specs=(grid, grid, grid, grid, grid, grid, grid, P(), P(), P(), P(), P(), P(), grid),
        out_specs=(grid, P(), P(), P(), P(), P(), P(), grid),
        check_vma=False,
    )
```
